256 devices in a mesh: row: 8 (over z_hi, y), col: 16 (over x, z_lo), rep: 2 (over core).
Axes of the slice: x: 4, y: 4, z: 8 (z_hi: 2, z_lo: 4; z = z_hi * 4 + z_lo), core: 2. Of those that a mesh axis runs over, the one named last changes fastest.
Arguments:
- ancestor_inverse: float32 [16384, 16384], P('row', 'col'), may hold values from -6 to 6
- tile_structure: int32 [128, 128], P('row', 'col'), may hold values from 0 to 1, as said below
- factor: float32 [16384, 512], P(('row', 'col')), may hold values from -0.046875 to 0.046875
- factor_normalizer: float32 [512, 512], replicated, may hold values from -1 to 1, as said below
- pivot_inverse: float32 [512, 512], P(None, 'rep'), may hold values from -6 to 6, as said below
Outputs:
- ancestor_columns: float32 [16384, 512], P(('row', 'col'), 'rep')
- diag_block: float32 [512, 512], P(None, 'rep')
The draws below stay inside these ranges and needn't reach their ends.
Inputs may be any that keep to these rules, and one draw needn't show every extreme that they name: `tile_structure`: symmetric, with ones on the diagonal. `factor_normalizer`: lower triangular with ones on its diagonal. `pivot_inverse`: symmetric.
All inputs are finite; a program needn't handle non-finite values.
Results may differ from the reference program's by a relative error of at most 0.000078.
Values sent between devices are 32-bit elements; how exact they have to be, the bound alone decides.
A program may use at most 64 MiB of HBM per device.

```python
import jax
import jax.numpy as jnp
from jax import lax

WIDTH = 512
TILE = 128
TILES = 128
ROWS = 16384


def draw_tile_structure(key, part):
    raw_bits = jax.random.randint(key, (TILES, TILES), 0, 2, dtype=jnp.int32)
    upper_part = jnp.triu(raw_bits, 1)
    return upper_part + upper_part.T + jnp.eye(TILES, dtype=jnp.int32)


def draw_factor_normalizer(key, part):
    inner_key = jax.random.fold_in(key, 11)
    entries = jnp.clip(jax.random.normal(inner_key, (WIDTH, WIDTH), jnp.float32), -4.0, 4.0)
    lower_part = jnp.tril(entries, -1) * (0.8 / jnp.sqrt(jnp.float32(WIDTH)))
    return lower_part + jnp.eye(WIDTH, dtype=jnp.float32)


def draw_pivot_inverse(key, part):
    inner_key = jax.random.fold_in(key, 23)
    entries = jnp.clip(jax.random.normal(inner_key, (WIDTH, WIDTH), jnp.float32), -4.0, 4.0)
    return (entries + entries.T) * 0.7071


def steps_of(own_key, dims, shards, low, largest):
    gain, own = 1.0, jax.random.fold_in(own_key, 6)
    for position, parts in shards:
        heights = jnp.exp(jax.random.uniform(jax.random.fold_in(own, position), (parts,), jnp.float32, low / len(shards), largest / len(shards)))
        gain = gain * jnp.repeat(heights, dims[position] // parts).reshape([-1 if axis == position else 1 for axis in range(len(dims))])
    return gain


def centred(own_key, shape, deviation, bound, cuts=(), held_as=jnp.bfloat16):
    gain = steps_of(own_key, shape, cuts, -0.22, 0.18) if cuts else 1.0
    array = jax.random.normal(own_key, shape, jnp.float32) * deviation * gain
    return jnp.minimum(jnp.maximum(array, -bound), bound).astype(held_as)


def setup_inputs(seed: int = 0) -> dict:
    keys = jax.random.split(jax.random.key(seed), 6)
    ancestor_inverse = centred(keys[0], (ROWS, ROWS), 1.0, 6.0, ((0, 8), (1, 16)), jnp.float32)
    tile_structure = draw_tile_structure(jax.random.fold_in(keys[5], 71), 0)
    factor = centred(keys[2], (ROWS, WIDTH), ROWS ** -0.5, 0.046875, ((0, 128),), jnp.float32)
    factor_normalizer = draw_factor_normalizer(jax.random.fold_in(keys[5], 71), 0)
    pivot_inverse = draw_pivot_inverse(jax.random.fold_in(keys[5], 71), 0)
    return {"ancestor_inverse": ancestor_inverse, "tile_structure": tile_structure, "factor": factor, "factor_normalizer": factor_normalizer, "pivot_inverse": pivot_inverse}


def reference(ancestor_inverse, tile_structure, factor, factor_normalizer, pivot_inverse):
    normed = jnp.dot(factor, factor_normalizer, precision=lax.Precision.HIGHEST, preferred_element_type=jnp.float32)

    def one_tile(index):
        inverse_rows = lax.dynamic_slice_in_dim(ancestor_inverse, index * TILE, TILE, 0)
        tile_marks = lax.dynamic_slice_in_dim(tile_structure, index, 1, 0).astype(jnp.float32)
        masked = (inverse_rows.reshape(TILE, TILES, TILE) * tile_marks.reshape(1, TILES, 1)).reshape(TILE, ROWS)
        return -jnp.dot(masked, normed, precision=lax.Precision.HIGHEST, preferred_element_type=jnp.float32)

    ancestor_columns = lax.map(one_tile, jnp.arange(TILES, dtype=jnp.int32)).reshape(ROWS, WIDTH)
    coupling = lax.dot_general(normed, ancestor_columns, (((0,), (0,)), ((), ())), precision=lax.Precision.HIGHEST, preferred_element_type=jnp.float32)
    diag_block = pivot_inverse - 0.5 * (coupling + coupling.T)
    return ancestor_columns, diag_block
```

```python
import jax
import jax.numpy as jnp
from jax import lax
from jax.experimental import pallas as pl
from jax.experimental.pallas import tpu as pltpu
from jax.sharding import PartitionSpec as P

F32 = jnp.float32
BF16 = jnp.bfloat16
MESH = pl.DeviceIdType.MESH


def split(value):
    high = value.astype(BF16)
    return high, (value - high.astype(F32)).astype(BF16)


def dot(left, right):
    return jnp.dot(left, right, preferred_element_type=F32)


def dot3(left, right):
    lh, ll = left
    rh, rl = right
    return dot(lh, rh) + (dot(lh, rl) + dot(ll, rh))


def kernel(
    tiles, a_hbm, f_hbm, n_hbm, y_out, s_out,
    af, ah, al, fac, nrm, nown, nth, ntl, xf, xc, p, gin, rin, zc, zin, yb, cp, win, tv, uin, cf, ein,
    a_sem, i_sem, s1s, s1r, ys, yr, xs, xr, zs, zr, ws, wr, us, ur, gs, gr, es, er,
):
    row, col, rep = (lax.axis_index(name) for name in ("row", "col", "rep"))
    tile, width = fac.shape
    half = width // 2
    part = half // 2
    quad = 4 * tile
    chunk = width // 16
    x, z_lo, z_hi, y = col // 4, col % 4, row // 4, row % 4
    z = z_hi * 4 + z_lo
    sent = []

    def place(px, py, pz):
        return (pz // 4 * 4 + py, px * 4 + pz % 4, rep)

    def send(src, dst, send_sem, recv_sem, device):
        copy = pltpu.make_async_remote_copy(
            src_ref=src, dst_ref=dst, send_sem=send_sem, recv_sem=recv_sem,
            device_id=device, device_id_type=MESH,
        )
        copy.start()
        sent.append(copy)

    def arrived(dst, sem):
        pltpu.make_async_copy(dst, dst, sem).wait()

    load_f = pltpu.make_async_copy(f_hbm, fac, i_sem.at[0])
    load_n = pltpu.make_async_copy(n_hbm, nrm, i_sem.at[1])
    load_f.start()
    load_n.start()

    def rows_of(a):
        return pl.ds(pl.multiple_of(a * tile, tile), tile)

    for a in range(16):
        pltpu.make_async_copy(a_hbm.at[rows_of(a)], af.at[rows_of(a)], a_sem.at[a]).start()

    barrier = pltpu.get_barrier_semaphore()
    for dx in range(4):
        for dy in range(4):
            if dx or dy:
                pl.semaphore_signal(barrier, inc=1, device_id=place((x + dx) % 4, (y + dy) % 4, z), device_id_type=MESH)
    for dz in range(1, 8):
        pl.semaphore_signal(barrier, inc=1, device_id=place(x, y, (z + dz) % 8), device_id_type=MESH)
    pl.semaphore_signal(barrier, inc=1, device_id=(row, col, 1 - rep), device_id_type=MESH)
    for slot in range(2):
        from_row, from_col = col // 2, col % 2 * 8 + y * 2 + slot
        mine = jnp.logical_and(from_row == row, from_col == col)

        @pl.when(jnp.logical_not(mine))
        def _():
            pl.semaphore_signal(barrier, inc=1, device_id=(from_row, from_col, rep), device_id_type=MESH)

    load_f.wait()
    load_n.wait()
    normed = dot3(split(fac[...]), split(nrm[...]))
    fac[...] = normed
    for q in range(2):
        nown[q] = fac[:, pl.ds(pl.multiple_of(rep * half + q * part, part), part)]

    kth = col % 8
    to_col = 2 * row + col // 8
    stays = jnp.logical_and(to_col == col, kth // 2 == y)
    pl.semaphore_wait(barrier, 15 + 7 + 1 + 2 - stays.astype(jnp.int32))
    landing = pl.ds(pl.multiple_of(kth * tile, tile), tile)
    first = []
    for q in range(2):
        for zh in range(2):
            to_row = zh * 4 + kth // 2
            mine = jnp.logical_and(to_row == row, to_col == col)
            copy = pltpu.make_async_remote_copy(
                src_ref=nown.at[q], dst_ref=xf.at[q, landing], send_sem=s1s.at[q, zh], recv_sem=s1r.at[q, kth % 2],
                device_id=(to_row, to_col, rep), device_id_type=MESH,
            )
            first.append((copy, mine))

            @pl.when(jnp.logical_not(mine))
            def _():
                copy.start()

            @pl.when(mine)
            def _():
                pltpu.make_async_copy(nown.at[q], xf.at[q, landing], s1r.at[q, kth % 2]).start()

    def mask_rows(a, carry):
        pltpu.make_async_copy(a_hbm.at[rows_of(a)], af.at[rows_of(a)], a_sem.at[a]).wait()
        for b in range(8):
            columns = slice(b * tile, (b + 1) * tile)
            high, low = split(af[rows_of(a), columns] * tiles[a, b].astype(F32))
            ah[rows_of(a), columns] = high
            al[rows_of(a), columns] = low
        return carry

    def y_exchange(q):
        for slot in range(2):
            arrived(xf.at[q, rows_of(y * 2 + slot)], s1r.at[q, slot])
        pair = pl.ds(pl.multiple_of(y * 2 * tile, 2 * tile), 2 * tile)
        for dy in (1, 3, 2):
            send(xf.at[q, pair], xf.at[q, pair], ys.at[q, dy - 1], yr.at[q, dy - 1], place(x, (y + dy) % 4, z))

    transposed = fac[...].T
    nth[...], ntl[...] = split(transposed)
    lax.fori_loop(0, 4, mask_rows, 0)
    y_exchange(0)
    lax.fori_loop(4, 8, mask_rows, 0)
    y_exchange(1)
    lax.fori_loop(8, 16, mask_rows, 0)

    def x_ready(q):
        for dy in range(1, 4):
            pair = pl.ds(pl.multiple_of((y + 4 - dy) % 4 * 2 * tile, 2 * tile), 2 * tile)
            arrived(xf.at[q, pair], yr.at[q, dy - 1])
        high, low = split(xf[q])
        xc[q, :, :part] = high
        xc[q, :, part:] = low

    xp, xo, xm = (x + 1) % 4, (x + 2) % 4, (x + 3) % 4

    def piece(block, side):
        return pl.ds(pl.multiple_of(block * quad + side * 2 * tile, 2 * tile), 2 * tile)

    sides = [slice(0, 2 * tile), slice(2 * tile, quad)]

    def product(q, block, side):
        rows = piece(block, side)
        both = dot(ah[rows, :], xc[q])
        p[q, rows, :] = both[:, :part] + (both[:, part:] + dot(al[rows, :], xc[q, :, :part]))

    def x_send(q, index, block, side, target, dst):
        send(p.at[q, piece(block, side)], dst, xs.at[q, index], xr.at[q, index], place(target, y, z))

    def products(q):
        x_ready(q)
        product(q, xo, 0)
        x_send(q, 0, xo, 0, xp, gin.at[q, 0])
        product(q, xo, 1)
        x_send(q, 1, xo, 1, xm, gin.at[q, 1])
        product(q, xp, 1)
        x_send(q, 2, xp, 1, xp, rin.at[q, 0, sides[1]])
        product(q, xm, 0)
        x_send(q, 3, xm, 0, xm, rin.at[q, 1, sides[0]])
        product(q, xp, 0)
        product(q, xm, 1)
        product(q, x, 0)
        product(q, x, 1)

    def x_pass_on(q):
        arrived(gin.at[q, 0], xr.at[q, 0])
        p[q, piece(xp, 0), :] += gin[q, 0]
        x_send(q, 4, xp, 0, xp, rin.at[q, 0, sides[0]])
        arrived(gin.at[q, 1], xr.at[q, 1])
        p[q, piece(xm, 1), :] += gin[q, 1]
        x_send(q, 5, xm, 1, xm, rin.at[q, 1, sides[1]])

    def z_send(q):
        arrived(rin.at[q, 0, sides[1]], xr.at[q, 2])
        arrived(rin.at[q, 1, sides[0]], xr.at[q, 3])
        arrived(rin.at[q, 0, sides[0]], xr.at[q, 4])
        arrived(rin.at[q, 1, sides[1]], xr.at[q, 5])
        for side in range(2):
            zc[q, sides[side]] = p[q, piece(x, side), :] + (rin[q, 0, sides[side]] + rin[q, 1, sides[side]])
        for dz in (2, 1, 3):
            to = (z_lo + dz) % 4
            send(zc.at[q, rows_of(to)], zin.at[q, dz - 1], zs.at[q, dz - 1], zr.at[q, dz - 1], place(x, y, z_hi * 4 + to))

    def plane():
        return [(dx, dy, dx * 4 + dy - 1) for dx in range(4) for dy in range(4) if dx or dy]

    def chunk_rows(index):
        return pl.ds(pl.multiple_of(index * chunk, chunk), chunk)

    def couple(q):
        total = zc[q, rows_of(z_lo), :]
        for dz in range(1, 4):
            arrived(zin.at[q, dz - 1], zr.at[q, dz - 1])
            total += zin[q, dz - 1]
        total = -total
        y_out[:, q * part : (q + 1) * part] = total
        cp[q] = dot3((nth[...], ntl[...]), split(total))
        for dx, dy, slot in plane():
            tx, ty = (x + dx) % 4, (y + dy) % 4
            send(cp.at[q, chunk_rows(tx * 4 + ty)], win.at[q, slot], ws.at[q, slot], wr.at[q, slot], place(tx, ty, z))

    own = x * 4 + y

    def z_share(q):
        total = cp[q, chunk_rows(own), :]
        for _, _, slot in plane():
            arrived(win.at[q, slot], wr.at[q, slot])
            total += win[q, slot]
        uin[q, z] = total
        tv[q] = total
        for dz in (4, 3, 5, 2, 6, 1, 7):
            send(tv.at[q], uin.at[q, z], us.at[q, dz - 1], ur.at[q, z], place(x, y, (z + dz) % 8))

    def gather(q):
        for dz in range(1, 8):
            source = (z + dz) % 8
            arrived(uin.at[q, source], ur.at[q, source])
        total = uin[q, 0]
        for source in range(1, 8):
            total += uin[q, source]
        cf[q, chunk_rows(own), :] = total
        for dx, dy, slot in plane():
            to = place((x + dx) % 4, (y + dy) % 4, z)
            send(cf.at[q, chunk_rows(own)], cf.at[q, chunk_rows(own)], gs.at[q, slot], gr.at[q, slot], to)

    mine_rows = pl.ds(pl.multiple_of(rep * half, half), half)
    other_rows = pl.ds(pl.multiple_of((1 - rep) * half, half), half)

    def exchange(q):
        for dx, dy, slot in plane():
            source = (x + 4 - dx) % 4 * 4 + (y + 4 - dy) % 4
            arrived(cf.at[q, chunk_rows(source)], gr.at[q, slot])
        send(cf.at[q, other_rows], ein.at[q], es.at[q], er.at[q], (row, col, 1 - rep))

    products(0)
    x_pass_on(0)
    products(1)
    z_send(0)
    x_pass_on(1)
    couple(0)
    z_send(1)
    z_share(0)
    couple(1)
    gather(0)
    z_share(1)
    gather(1)
    exchange(0)
    exchange(1)
    block = jnp.concatenate([cf[0, mine_rows, :], cf[1, mine_rows, :]], 1)
    s_out[mine_rows, :] = 0.5 * (block + block.T)
    for q in range(2):
        arrived(ein.at[q], er.at[q])
    mirrored = jnp.concatenate([ein[0].T, ein[1].T], 0)
    s_out[other_rows, :] = 0.5 * (jnp.concatenate([cf[0, other_rows, :], cf[1, other_rows, :]], 1) + mirrored)
    for copy, mine in first:

        @pl.when(jnp.logical_not(mine))
        def _():
            copy.wait_send()

    for copy in sent:
        copy.wait_send()


def body(ancestor_inverse, tile_structure, factor, factor_normalizer, pivot_inverse):
    tile, width = factor.shape
    part = width // 4
    rows, columns = ancestor_inverse.shape
    chunk = width // 16
    vmem, dma = pltpu.VMEM, pltpu.SemaphoreType.DMA
    anywhere = pl.BlockSpec(memory_space=pl.ANY)
    in_vmem = pl.BlockSpec(memory_space=pltpu.VMEM)
    ancestor_columns, symmetric = pl.pallas_call(
        kernel,
        out_shape=(
            jax.ShapeDtypeStruct((tile, 2 * part), F32),
            jax.ShapeDtypeStruct((width, 2 * part), F32),
        ),
        in_specs=[pl.BlockSpec(memory_space=pltpu.SMEM), anywhere, anywhere, anywhere],
        out_specs=(in_vmem, in_vmem),
        scratch_shapes=[
            vmem((rows, columns), F32),
            vmem((rows, columns), BF16),
            vmem((rows, columns), BF16),
            vmem((tile, width), F32),
            vmem((width, width), F32),
            vmem((2, tile, part), F32),
            vmem((width, tile), BF16),
            vmem((width, tile), BF16),
            vmem((2, columns, part), F32),
            vmem((2, columns, 2 * part), BF16),
            vmem((2, rows, part), F32),
            vmem((2, 2, 2 * tile, part), F32),
            vmem((2, 2, 4 * tile, part), F32),
            vmem((2, 4 * tile, part), F32),
            vmem((2, 3, tile, part), F32),
            vmem((2, tile, part), F32),
            vmem((2, width, part), F32),
            vmem((2, 15, chunk, part), F32),
            vmem((2, chunk, part), F32),
            vmem((2, 8, chunk, part), F32),
            vmem((2, width, part), F32),
            vmem((2, 2 * part, part), F32),
            dma((16,)),
            dma((2,)),
            dma((2, 2)),
            dma((2, 2)),
            dma((2, 3)),
            dma((2, 3)),
            dma((2, 6)),
            dma((2, 6)),
            dma((2, 3)),
            dma((2, 3)),
            dma((2, 15)),
            dma((2, 15)),
            dma((2, 7)),
            dma((2, 8)),
            dma((2, 15)),
            dma((2, 15)),
            dma((2,)),
            dma((2,)),
        ],
        compiler_params=pltpu.CompilerParams(collective_id=0, has_side_effects=True, vmem_limit_bytes=48 * 1024 * 1024),
    )(tile_structure, ancestor_inverse, factor, factor_normalizer)
    return ancestor_columns, pivot_inverse - symmetric


def solution(mesh):
    return jax.shard_map(
        body,
        mesh=mesh,
        in_specs=(P("row", "col"), P("row", "col"), P(("row", "col"), None), P(), P(None, "rep")),
        out_specs=(P(("row", "col"), "rep"), P(None, "rep")),
        check_vma=False,
    )
```

```python
import jax
import jax.numpy as jnp
from jax import lax
from jax.experimental import pallas as pl
from jax.experimental.pallas import tpu as pltpu
from jax.sharding import PartitionSpec as P

F32 = jnp.float32
BF16 = jnp.bfloat16
MESH = pl.DeviceIdType.MESH


def split(value):
    high = value.astype(BF16)
    return high, (value - high.astype(F32)).astype(BF16)


def dot(left, right):
    return jnp.dot(left, right, preferred_element_type=F32)


def dot3(left, right):
    lh, ll = left
    rh, rl = right
    return dot(lh, rh) + (dot(lh, rl) + dot(ll, rh))


def kernel(
    tiles, a_hbm, f_hbm, n_hbm, y_out, s_out,
    af, ah, al, fac, nrm, nown, nth, ntl, xf, xc, p, gin, rin, zc, zin, yb, cp, win, tv, uin, cf, ein,
    bn, nz, a_sem, i_sem, bs, br, ns, nr, ms, mr, s1s, s1r, ys, yr, xs, xr, zs, zr, ws, wr, us, ur, gs, gr, es, er,
):
    row, col, rep = (lax.axis_index(name) for name in ("row", "col", "rep"))
    tile, width = fac.shape
    half = width // 2
    part = half // 2
    quad = 4 * tile
    chunk = width // 16
    x, z_lo, z_hi, y = col // 4, col % 4, row // 4, row % 4
    z = z_hi * 4 + z_lo
    sent = []

    def place(px, py, pz):
        return (pz // 4 * 4 + py, px * 4 + pz % 4, rep)

    def send(src, dst, send_sem, recv_sem, device):
        copy = pltpu.make_async_remote_copy(
            src_ref=src, dst_ref=dst, send_sem=send_sem, recv_sem=recv_sem,
            device_id=device, device_id_type=MESH,
        )
        copy.start()
        sent.append(copy)

    def arrived(dst, sem):
        pltpu.make_async_copy(dst, dst, sem).wait()

    load_f = pltpu.make_async_copy(f_hbm, fac, i_sem.at[0])
    load_f.start()
    slices = [rep * 2, rep * 2 + 1, 2 - rep * 2, 3 - rep * 2]

    def slice_of(index):
        return pl.ds(pl.multiple_of(slices[index] * part, part), part)

    load_n = [pltpu.make_async_copy(n_hbm.at[:, slice_of(i)], nrm.at[i], i_sem.at[1 + i]) for i in range(4)]
    for load in load_n:
        load.start()

    def rows_of(a):
        return pl.ds(pl.multiple_of(a * tile, tile), tile)

    for a in range(16):
        pltpu.make_async_copy(a_hbm.at[rows_of(a)], af.at[rows_of(a)], a_sem.at[a]).start()

    barrier = pltpu.get_barrier_semaphore()
    for dx in range(4):
        for dy in range(4):
            near = place((x + dx) % 4, (y + dy) % 4, z)
            if dx or dy:
                pl.semaphore_signal(barrier, inc=1, device_id=near, device_id_type=MESH)
            pl.semaphore_signal(barrier, inc=1, device_id=(near[0], near[1], 1 - rep), device_id_type=MESH)
    for dz in range(1, 8):
        pl.semaphore_signal(barrier, inc=1, device_id=place(x, y, (z + dz) % 8), device_id_type=MESH)
    for slot in range(8):
        from_row, from_col = row, col % 2 * 8 + slot
        mine = jnp.logical_and(from_row == row, from_col == col)

        @pl.when(jnp.logical_not(mine))
        def _():
            pl.semaphore_signal(barrier, inc=1, device_id=(from_row, from_col, rep), device_id_type=MESH)

    load_f.wait()

    def normed(index):
        load_n[index].wait()
        value = dot3(split(fac[...]), split(nrm[index]))
        if index < 2:
            nown[index] = value
        return value

    def keep_transposed(index, value):
        high, low = split(value.T)
        nth[slice_of(index), rows_of(z_lo)] = high
        ntl[slice_of(index), rows_of(z_lo)] = low

    own_slices = pl.ds(rep * 2, 2)

    def normed_share():
        for dz in (2, 1, 3):
            to = place(x, y, z_hi * 4 + (z_lo + dz) % 4)
            send(nown, nz.at[z_lo, own_slices], ns.at[dz - 1], nr.at[z_lo], to)

    def normed_forward():
        for dz in range(1, 4):
            peer = (z_lo + dz) % 4
            arrived(nz.at[peer, own_slices], nr.at[peer])
            send(nz.at[peer, own_slices], nz.at[peer, own_slices], ms.at[dz - 1], mr.at[peer], (row, col, 1 - rep))

    def normed_ready():
        for dz in range(1, 4):
            peer = (z_lo + dz) % 4
            arrived(nz.at[peer, pl.ds(2 - rep * 2, 2)], mr.at[peer])
            for index in range(4):
                high, low = split(nz[peer, index].T)
                nth[index * part : (index + 1) * part, rows_of(peer)] = high
                ntl[index * part : (index + 1) * part, rows_of(peer)] = low

    value = normed(0)

    kth = col % 8
    to_col = 2 * row + col // 8
    for ty in range(1, 4):
        to = place(x, (y + ty) % 4, (z + 4) % 8)
        pl.semaphore_signal(barrier, inc=1, device_id=to, device_id_type=MESH)
    pl.semaphore_wait(barrier, 31 + 7 + 3 + 8 - (col % 2 == col // 8).astype(jnp.int32))
    piece_rows = tile // 4
    first = []

    def row_send(q):
        for zh in range(2):
            for ty in range(4):
                if zh or ty:
                    to_y, to_z = (y + ty) % 4, (z + zh * 4) % 8
                    source = nown.at[q, pl.ds(pl.multiple_of(to_y * piece_rows, piece_rows), piece_rows)]
                    send(source, bn.at[q, row], bs.at[q, zh * 4 + ty - 1], br.at[q, row], place(x, to_y, to_z))
        bn[q, row] = nown[q, pl.ds(pl.multiple_of(y * piece_rows, piece_rows), piece_rows)]

    def plane_send(q):
        for shift in range(8):
            owner = (col // 2 + shift) % 8

            @pl.when(owner != row)
            def _():
                arrived(bn.at[q, owner], br.at[q, owner])

            target = 2 * owner + col // 8
            mine = target == col
            copy = pltpu.make_async_remote_copy(
                src_ref=bn.at[q, owner], dst_ref=xf.at[q, kth, y], send_sem=s1s.at[q, shift], recv_sem=s1r.at[q, kth],
                device_id=(row, target, rep), device_id_type=MESH,
            )
            first.append((copy, mine))

            @pl.when(jnp.logical_not(mine))
            def _():
                copy.start()

            @pl.when(mine)
            def _():
                pltpu.make_async_copy(bn.at[q, owner], xf.at[q, kth, y], s1r.at[q, kth]).start()

    def mask_rows(a, carry):
        pltpu.make_async_copy(a_hbm.at[rows_of(a)], af.at[rows_of(a)], a_sem.at[a]).wait()
        for b in range(8):
            columns = slice(b * tile, (b + 1) * tile)
            high, low = split(af[rows_of(a), columns] * tiles[a, b].astype(F32))
            ah[rows_of(a), columns] = high
            al[rows_of(a), columns] = low
        return carry

    def y_exchange(q):
        for slot in range(8):
            arrived(xf.at[q, slot, y], s1r.at[q, slot])
        for dy in (1, 3, 2):
            send(xf.at[q, :, y], xf.at[q, :, y], ys.at[q, dy - 1], yr.at[q, dy - 1], place(x, (y + dy) % 4, z))

    row_send(0)
    keep_transposed(0, value)
    for index in range(1, 4):
        keep_transposed(index, normed(index))
    lax.fori_loop(0, 6, mask_rows, 0)
    plane_send(0)
    row_send(1)
    lax.fori_loop(6, 12, mask_rows, 0)
    y_exchange(0)
    lax.fori_loop(12, 16, mask_rows, 0)
    plane_send(1)
    y_exchange(1)
    normed_share()

    def x_ready(q):
        for dy in range(1, 4):
            arrived(xf.at[q, :, (y + 4 - dy) % 4], yr.at[q, dy - 1])
        high, low = split(xf[q].reshape(8 * tile, part))
        xc[q, :, :part] = high
        xc[q, :, part:] = low

    xp, xo, xm = (x + 1) % 4, (x + 2) % 4, (x + 3) % 4

    def piece(block, side):
        return pl.ds(pl.multiple_of(block * quad + side * 2 * tile, 2 * tile), 2 * tile)

    sides = [slice(0, 2 * tile), slice(2 * tile, quad)]

    def product(q, block, side):
        rows = piece(block, side)
        both = dot(ah[rows, :], xc[q])
        p[q, rows, :] = both[:, :part] + (both[:, part:] + dot(al[rows, :], xc[q, :, :part]))

    def x_send(q, index, block, side, target, dst):
        send(p.at[q, piece(block, side)], dst, xs.at[q, index], xr.at[q, index], place(target, y, z))

    def products(q):
        x_ready(q)
        product(q, xo, 0)
        x_send(q, 0, xo, 0, xp, gin.at[q, 0])
        product(q, xo, 1)
        x_send(q, 1, xo, 1, xm, gin.at[q, 1])
        product(q, xp, 1)
        x_send(q, 2, xp, 1, xp, rin.at[q, 0, sides[1]])
        product(q, xm, 0)
        x_send(q, 3, xm, 0, xm, rin.at[q, 1, sides[0]])
        product(q, xp, 0)
        product(q, xm, 1)
        product(q, x, 0)
        product(q, x, 1)

    def x_pass_on(q):
        arrived(gin.at[q, 0], xr.at[q, 0])
        p[q, piece(xp, 0), :] += gin[q, 0]
        x_send(q, 4, xp, 0, xp, rin.at[q, 0, sides[0]])
        arrived(gin.at[q, 1], xr.at[q, 1])
        p[q, piece(xm, 1), :] += gin[q, 1]
        x_send(q, 5, xm, 1, xm, rin.at[q, 1, sides[1]])

    def z_send(q):
        arrived(rin.at[q, 0, sides[1]], xr.at[q, 2])
        arrived(rin.at[q, 1, sides[0]], xr.at[q, 3])
        arrived(rin.at[q, 0, sides[0]], xr.at[q, 4])
        arrived(rin.at[q, 1, sides[1]], xr.at[q, 5])
        for side in range(2):
            zc[q, sides[side]] = p[q, piece(x, side), :] + (rin[q, 0, sides[side]] + rin[q, 1, sides[side]])
        for dz in (2, 1, 3):
            to = (z_lo + dz) % 4
            send(zc.at[q, rows_of(to)], zin.at[q, dz - 1], zs.at[q, dz - 1], zr.at[q, dz - 1], place(x, y, z_hi * 4 + to))

    def plane():
        return [(dx, dy, dx * 4 + dy - 1) for dx in range(4) for dy in range(4) if dx or dy]

    def chunk_rows(index):
        return pl.ds(pl.multiple_of(index * chunk, chunk), chunk)

    def couple(q):
        cp[q] = dot3((nth[...], ntl[...]), split(-zc[q]))
        for dx, dy, slot in plane():
            tx, ty = (x + dx) % 4, (y + dy) % 4
            send(cp.at[q, chunk_rows(tx * 4 + ty)], win.at[q, slot], ws.at[q, slot], wr.at[q, slot], place(tx, ty, z))

    def columns_out(q):
        total = zc[q, rows_of(z_lo), :]
        for dz in range(1, 4):
            arrived(zin.at[q, dz - 1], zr.at[q, dz - 1])
            total += zin[q, dz - 1]
        y_out[:, q * part : (q + 1) * part] = -total

    own = x * 4 + y

    def z_share(q):
        total = cp[q, chunk_rows(own), :]
        for _, _, slot in plane():
            arrived(win.at[q, slot], wr.at[q, slot])
            total += win[q, slot]
        uin[q, z] = total
        tv[q] = total
        for dz in (4, 3, 5, 2, 6, 1, 7):
            send(tv.at[q], uin.at[q, z], us.at[q, dz - 1], ur.at[q, z], place(x, y, (z + dz) % 8))

    def gather(q):
        for dz in range(1, 8):
            source = (z + dz) % 8
            arrived(uin.at[q, source], ur.at[q, source])
        total = uin[q, 0]
        for source in range(1, 8):
            total += uin[q, source]
        cf[q, chunk_rows(own), :] = total
        for dx, dy, slot in plane():
            to = place((x + dx) % 4, (y + dy) % 4, z)
            send(cf.at[q, chunk_rows(own)], cf.at[q, chunk_rows(own)], gs.at[q, slot], gr.at[q, slot], to)

        @pl.when(crosses)
        def _():
            for copy in cross_copies(q):
                copy.start()

    crosses = own // 8 != rep

    def cross_copies(q):
        copies = []
        for dx in range(4):
            for dy in range(4):
                to = place((x + dx) % 4, (y + dy) % 4, z)
                copies.append(
                    pltpu.make_async_remote_copy(
                        src_ref=cf.at[q, chunk_rows(own)], dst_ref=ein.at[q, chunk_rows(own % 8)],
                        send_sem=es.at[q, dx * 4 + dy], recv_sem=er.at[q, own % 8],
                        device_id=(to[0], to[1], 1 - rep), device_id_type=MESH,
                    )
                )
        return copies

    mine_rows = pl.ds(pl.multiple_of(rep * half, half), half)
    other_rows = pl.ds(pl.multiple_of((1 - rep) * half, half), half)

    def finished(q):
        for dx, dy, slot in plane():
            source = (x + 4 - dx) % 4 * 4 + (y + 4 - dy) % 4
            arrived(cf.at[q, chunk_rows(source)], gr.at[q, slot])
        for slot in range(8):
            arrived(ein.at[q, chunk_rows(slot)], er.at[q, slot])

    products(0)
    x_pass_on(0)
    products(1)
    normed_forward()
    z_send(0)
    x_pass_on(1)
    normed_ready()
    couple(0)
    z_send(1)
    couple(1)
    z_share(0)
    z_share(1)
    gather(0)
    columns_out(0)
    gather(1)
    columns_out(1)
    finished(0)
    finished(1)
    block = jnp.concatenate([cf[0, mine_rows, :], cf[1, mine_rows, :]], 1)
    s_out[mine_rows, :] = 0.5 * (block + block.T)
    mirrored = jnp.concatenate([ein[0].T, ein[1].T], 0)
    s_out[other_rows, :] = 0.5 * (jnp.concatenate([cf[0, other_rows, :], cf[1, other_rows, :]], 1) + mirrored)
    for copy, mine in first:

        @pl.when(jnp.logical_not(mine))
        def _():
            copy.wait_send()

    @pl.when(crosses)
    def _():
        for q in range(2):
            for copy in cross_copies(q):
                copy.wait_send()

    for copy in sent:
        copy.wait_send()


def body(ancestor_inverse, tile_structure, factor, factor_normalizer, pivot_inverse):
    tile, width = factor.shape
    part = width // 4
    rows, columns = ancestor_inverse.shape
    chunk = width // 16
    vmem, dma = pltpu.VMEM, pltpu.SemaphoreType.DMA
    anywhere = pl.BlockSpec(memory_space=pl.ANY)
    in_vmem = pl.BlockSpec(memory_space=pltpu.VMEM)
    ancestor_columns, symmetric = pl.pallas_call(
        kernel,
        out_shape=(
            jax.ShapeDtypeStruct((tile, 2 * part), F32),
            jax.ShapeDtypeStruct((width, 2 * part), F32),
        ),
        in_specs=[pl.BlockSpec(memory_space=pltpu.SMEM), anywhere, anywhere, anywhere],
        out_specs=(in_vmem, in_vmem),
        scratch_shapes=[
            vmem((rows, columns), F32),
            vmem((rows, columns), BF16),
            vmem((rows, columns), BF16),
            vmem((tile, width), F32),
            vmem((4, width, part), F32),
            vmem((2, tile, part), F32),
            vmem((width, 4 * tile), BF16),
            vmem((width, 4 * tile), BF16),
            vmem((2, 8, 4, tile // 4, part), F32),
            vmem((2, columns, 2 * part), BF16),
            vmem((2, rows, part), F32),
            vmem((2, 2, 2 * tile, part), F32),
            vmem((2, 2, 4 * tile, part), F32),
            vmem((2, 4 * tile, part), F32),
            vmem((2, 3, tile, part), F32),
            vmem((2, tile, part), F32),
            vmem((2, width, part), F32),
            vmem((2, 15, chunk, part), F32),
            vmem((2, chunk, part), F32),
            vmem((2, 8, chunk, part), F32),
            vmem((2, width, part), F32),
            vmem((2, 2 * part, part), F32),
            vmem((2, 8, tile // 4, part), F32),
            vmem((4, 4, tile, part), F32),
            dma((16,)),
            dma((5,)),
            dma((2, 7)),
            dma((2, 8)),
            dma((3,)),
            dma((4,)),
            dma((3,)),
            dma((4,)),
            dma((2, 8)),
            dma((2, 8)),
            dma((2, 3)),
            dma((2, 3)),
            dma((2, 6)),
            dma((2, 6)),
            dma((2, 3)),
            dma((2, 3)),
            dma((2, 15)),
            dma((2, 15)),
            dma((2, 7)),
            dma((2, 8)),
            dma((2, 15)),
            dma((2, 15)),
            dma((2, 16)),
            dma((2, 8)),
        ],
        compiler_params=pltpu.CompilerParams(collective_id=0, has_side_effects=True, vmem_limit_bytes=60 * 1024 * 1024),
    )(tile_structure, ancestor_inverse, factor, factor_normalizer)
    return ancestor_columns, pivot_inverse - symmetric


def solution(mesh):
    return jax.shard_map(
        body,
        mesh=mesh,
        in_specs=(P("row", "col"), P("row", "col"), P(("row", "col"), None), P(), P(None, "rep")),
        out_specs=(P(("row", "col"), "rep"), P(None, "rep")),
        check_vma=False,
    )
```

```python
import jax
import jax.numpy as jnp
from jax import lax
from jax.experimental import pallas as pl
from jax.experimental.pallas import tpu as pltpu
from jax.sharding import PartitionSpec as P

F32 = jnp.float32
BF16 = jnp.bfloat16
MESH = pl.DeviceIdType.MESH


def split(value):
    high = value.astype(BF16)
    return high, (value - high.astype(F32)).astype(BF16)


def dot(left, right):
    return jnp.dot(left, right, preferred_element_type=F32)


def dot3(left, right):
    lh, ll = left
    rh, rl = right
    return dot(lh, rh) + (dot(lh, rl) + dot(ll, rh))


def kernel(
    tiles, a_hbm, f_hbm, n_hbm, y_out, s_out,
    af, ah, al, fac, nrm, nown, nth, ntl, xf, xc, p, gin, rin, zc, zin, yb, cp, win, tv, uin, cf, ein,
    bn, nz, a_sem, i_sem, bs, br, ns, nr, ms, mr, s1s, s1r, ys, yr, xs, xr, zs, zr, ws, wr, us, ur, gs, gr, es, er,
):
    row, col, rep = (lax.axis_index(name) for name in ("row", "col", "rep"))
    tile, width = fac.shape
    half = width // 2
    part = half // 2
    quad = 4 * tile
    chunk = width // 16
    x, z_lo, z_hi, y = col // 4, col % 4, row // 4, row % 4
    z = z_hi * 4 + z_lo
    sent = []

    def place(px, py, pz):
        return (pz // 4 * 4 + py, px * 4 + pz % 4, rep)

    def send(src, dst, send_sem, recv_sem, device):
        copy = pltpu.make_async_remote_copy(
            src_ref=src, dst_ref=dst, send_sem=send_sem, recv_sem=recv_sem,
            device_id=device, device_id_type=MESH,
        )
        copy.start()
        sent.append(copy)

    def arrived(dst, sem):
        pltpu.make_async_copy(dst, dst, sem).wait()

    load_f = pltpu.make_async_copy(f_hbm, fac, i_sem.at[0])
    load_f.start()
    slices = [rep * 2, rep * 2 + 1, 2 - rep * 2, 3 - rep * 2]

    def slice_of(index):
        return pl.ds(pl.multiple_of(slices[index] * part, part), part)

    load_n = [pltpu.make_async_copy(n_hbm.at[:, slice_of(i)], nrm.at[i], i_sem.at[1 + i]) for i in range(4)]
    for load in load_n:
        load.start()

    def rows_of(a):
        return pl.ds(pl.multiple_of(a * tile, tile), tile)

    for a in range(16):
        pltpu.make_async_copy(a_hbm.at[rows_of(a)], af.at[rows_of(a)], a_sem.at[a]).start()

    barrier = pltpu.get_barrier_semaphore()
    for dx in range(4):
        for dy in range(4):
            near = place((x + dx) % 4, (y + dy) % 4, z)
            if dx or dy:
                pl.semaphore_signal(barrier, inc=1, device_id=near, device_id_type=MESH)
            pl.semaphore_signal(barrier, inc=1, device_id=(near[0], near[1], 1 - rep), device_id_type=MESH)
    for dz in range(1, 8):
        pl.semaphore_signal(barrier, inc=1, device_id=place(x, y, (z + dz) % 8), device_id_type=MESH)
    for slot in range(8):
        from_row, from_col = row, col % 2 * 8 + slot
        mine = jnp.logical_and(from_row == row, from_col == col)

        @pl.when(jnp.logical_not(mine))
        def _():
            pl.semaphore_signal(barrier, inc=1, device_id=(from_row, from_col, rep), device_id_type=MESH)

    load_f.wait()

    def normed(index):
        load_n[index].wait()
        value = dot3(split(fac[...]), split(nrm[index]))
        if index < 2:
            nown[index] = value
        return value

    def keep_transposed(index, value):
        high, low = split(value.T)
        nth[slice_of(index), rows_of(z_lo)] = high
        ntl[slice_of(index), rows_of(z_lo)] = low

    own_slices = pl.ds(rep * 2, 2)

    def normed_share():
        for dz in (2, 1, 3):
            to = place(x, y, z_hi * 4 + (z_lo + dz) % 4)
            send(nown, nz.at[z_lo, own_slices], ns.at[dz - 1], nr.at[z_lo], to)

    def normed_forward():
        for dz in range(1, 4):
            peer = (z_lo + dz) % 4
            arrived(nz.at[peer, own_slices], nr.at[peer])
            send(nz.at[peer, own_slices], nz.at[peer, own_slices], ms.at[dz - 1], mr.at[peer], (row, col, 1 - rep))

    def normed_ready():
        for dz in range(1, 4):
            peer = (z_lo + dz) % 4
            arrived(nz.at[peer, pl.ds(2 - rep * 2, 2)], mr.at[peer])
            for index in range(4):
                high, low = split(nz[peer, index].T)
                nth[index * part : (index + 1) * part, rows_of(peer)] = high
                ntl[index * part : (index + 1) * part, rows_of(peer)] = low

    value = normed(0)

    kth = col % 8
    to_col = 2 * row + col // 8
    for ty in range(1, 4):
        to = place(x, (y + ty) % 4, (z + 4) % 8)
        pl.semaphore_signal(barrier, inc=1, device_id=to, device_id_type=MESH)
    pl.semaphore_wait(barrier, 31 + 7 + 3 + 8 - (col % 2 == col // 8).astype(jnp.int32))
    piece_rows = tile // 4
    first = []

    def row_send(q):
        for zh in range(2):
            for ty in range(4):
                if zh or ty:
                    to_y, to_z = (y + ty) % 4, (z + zh * 4) % 8
                    source = nown.at[q, pl.ds(pl.multiple_of(to_y * piece_rows, piece_rows), piece_rows)]
                    send(source, bn.at[q, row], bs.at[q, zh * 4 + ty - 1], br.at[q, row], place(x, to_y, to_z))
        bn[q, row] = nown[q, pl.ds(pl.multiple_of(y * piece_rows, piece_rows), piece_rows)]

    def plane_send(q):
        for shift in range(8):
            owner = (col // 2 + shift) % 8

            @pl.when(owner != row)
            def _():
                arrived(bn.at[q, owner], br.at[q, owner])

            target = 2 * owner + col // 8
            mine = target == col
            copy = pltpu.make_async_remote_copy(
                src_ref=bn.at[q, owner], dst_ref=xf.at[q, kth, y], send_sem=s1s.at[q, shift], recv_sem=s1r.at[q, kth],
                device_id=(row, target, rep), device_id_type=MESH,
            )
            first.append((copy, mine))

            @pl.when(jnp.logical_not(mine))
            def _():
                copy.start()

            @pl.when(mine)
            def _():
                pltpu.make_async_copy(bn.at[q, owner], xf.at[q, kth, y], s1r.at[q, kth]).start()

    def mask_rows(a, carry):
        pltpu.make_async_copy(a_hbm.at[rows_of(a)], af.at[rows_of(a)], a_sem.at[a]).wait()
        marks = tiles[pl.ds(a, 1), :]
        for b in range(8):
            columns = slice(b * tile, (b + 1) * tile)
            high, low = split(af[rows_of(a), columns] * marks[:, b : b + 1])
            ah[rows_of(a), columns] = high
            al[rows_of(a), columns] = low
        return carry

    def y_exchange(q):
        for group in range(2):
            four = pl.ds(group * 4, 4)
            for slot in range(4):
                arrived(xf.at[q, group * 4 + slot, y], s1r.at[q, group * 4 + slot])
            for dy in (1, 3, 2):
                index = group * 3 + dy - 1
                send(xf.at[q, four, y], xf.at[q, four, y], ys.at[q, index], yr.at[q, index], place(x, (y + dy) % 4, z))

    row_send(0)
    keep_transposed(0, value)
    for index in range(1, 4):
        keep_transposed(index, normed(index))
    lax.fori_loop(0, 2, mask_rows, 0)
    row_send(1)
    lax.fori_loop(2, 7, mask_rows, 0)
    plane_send(0)
    lax.fori_loop(7, 13, mask_rows, 0)
    plane_send(1)
    y_exchange(0)
    lax.fori_loop(13, 16, mask_rows, 0)
    y_exchange(1)
    normed_share()

    def x_ready(q):
        for dy in range(1, 4):
            for group in range(2):
                arrived(xf.at[q, pl.ds(group * 4, 4), (y + 4 - dy) % 4], yr.at[q, group * 3 + dy - 1])
        high, low = split(xf[q].reshape(8 * tile, part))
        xc[q, :, :part] = high
        xc[q, :, part:] = low

    xp, xo, xm = (x + 1) % 4, (x + 2) % 4, (x + 3) % 4

    def piece(block, side):
        return pl.ds(pl.multiple_of(block * quad + side * 2 * tile, 2 * tile), 2 * tile)

    sides = [slice(0, 2 * tile), slice(2 * tile, quad)]

    def product(q, block, side):
        rows = piece(block, side)
        both = dot(ah[rows, :], xc[q])
        p[q, rows, :] = both[:, :part] + (both[:, part:] + dot(al[rows, :], xc[q, :, :part]))

    def x_send(q, index, block, side, target, dst):
        send(p.at[q, piece(block, side)], dst, xs.at[q, index], xr.at[q, index], place(target, y, z))

    def products(q):
        x_ready(q)
        product(q, xo, 0)
        x_send(q, 0, xo, 0, xp, gin.at[q, 0])
        product(q, xo, 1)
        x_send(q, 1, xo, 1, xm, gin.at[q, 1])
        product(q, xp, 1)
        x_send(q, 2, xp, 1, xp, rin.at[q, 0, sides[1]])
        product(q, xm, 0)
        x_send(q, 3, xm, 0, xm, rin.at[q, 1, sides[0]])
        product(q, xp, 0)
        product(q, xm, 1)
        product(q, x, 0)
        product(q, x, 1)

    def x_pass_on(q):
        arrived(gin.at[q, 0], xr.at[q, 0])
        p[q, piece(xp, 0), :] += gin[q, 0]
        x_send(q, 4, xp, 0, xp, rin.at[q, 0, sides[0]])
        arrived(gin.at[q, 1], xr.at[q, 1])
        p[q, piece(xm, 1), :] += gin[q, 1]
        x_send(q, 5, xm, 1, xm, rin.at[q, 1, sides[1]])

    def z_send(q):
        arrived(rin.at[q, 0, sides[1]], xr.at[q, 2])
        arrived(rin.at[q, 1, sides[0]], xr.at[q, 3])
        arrived(rin.at[q, 0, sides[0]], xr.at[q, 4])
        arrived(rin.at[q, 1, sides[1]], xr.at[q, 5])
        for side in range(2):
            zc[q, sides[side]] = p[q, piece(x, side), :] + (rin[q, 0, sides[side]] + rin[q, 1, sides[side]])
        for dz in (2, 1, 3):
            to = (z_lo + dz) % 4
            send(zc.at[q, rows_of(to)], zin.at[q, dz - 1], zs.at[q, dz - 1], zr.at[q, dz - 1], place(x, y, z_hi * 4 + to))

    def plane():
        return [(dx, dy, dx * 4 + dy - 1) for dx in range(4) for dy in range(4) if dx or dy]

    def chunk_rows(index):
        return pl.ds(pl.multiple_of(index * chunk, chunk), chunk)

    def couple(q):
        sums = split(-zc[q])
        for dx in (2, 1, 3, 0):
            tx = (x + dx) % 4
            rows = pl.ds(pl.multiple_of(tx * 4 * chunk, 4 * chunk), 4 * chunk)
            cp[q, rows, :] = dot3((nth[rows, :], ntl[rows, :]), sums)
            for dy in (2, 1, 3, 0):
                if dx or dy:
                    ty, slot = (y + dy) % 4, dx * 4 + dy - 1
                    source = cp.at[q, chunk_rows(tx * 4 + ty)]
                    send(source, win.at[q, slot], ws.at[q, slot], wr.at[q, slot], place(tx, ty, z))

    def columns_out(q):
        total = zc[q, rows_of(z_lo), :]
        for dz in range(1, 4):
            arrived(zin.at[q, dz - 1], zr.at[q, dz - 1])
            total += zin[q, dz - 1]
        y_out[:, q * part : (q + 1) * part] = -total

    own = x * 4 + y

    def z_share(q):
        total = cp[q, chunk_rows(own), :]
        for _, _, slot in plane():
            arrived(win.at[q, slot], wr.at[q, slot])
            total += win[q, slot]
        uin[q, z] = total
        tv[q] = total
        for dz in (4, 3, 5, 2, 6, 1, 7):
            send(tv.at[q], uin.at[q, z], us.at[q, dz - 1], ur.at[q, z], place(x, y, (z + dz) % 8))

    def gather(q):
        for dz in range(1, 8):
            source = (z + dz) % 8
            arrived(uin.at[q, source], ur.at[q, source])
        total = uin[q, 0]
        for source in range(1, 8):
            total += uin[q, source]
        cf[q, chunk_rows(own), :] = total
        for dx, dy, slot in plane():
            to = place((x + dx) % 4, (y + dy) % 4, z)
            send(cf.at[q, chunk_rows(own)], cf.at[q, chunk_rows(own)], gs.at[q, slot], gr.at[q, slot], to)

        @pl.when(crosses)
        def _():
            for copy in cross_copies(q):
                copy.start()

    crosses = own // 8 != rep

    def cross_copies(q):
        copies = []
        for dx in range(4):
            for dy in range(4):
                to = place((x + dx) % 4, (y + dy) % 4, z)
                copies.append(
                    pltpu.make_async_remote_copy(
                        src_ref=cf.at[q, chunk_rows(own)], dst_ref=ein.at[q, chunk_rows(own % 8)],
                        send_sem=es.at[q, dx * 4 + dy], recv_sem=er.at[q, own % 8],
                        device_id=(to[0], to[1], 1 - rep), device_id_type=MESH,
                    )
                )
        return copies

    mine_rows = pl.ds(pl.multiple_of(rep * half, half), half)
    other_rows = pl.ds(pl.multiple_of((1 - rep) * half, half), half)

    def finished(q):
        for dx, dy, slot in plane():
            source = (x + 4 - dx) % 4 * 4 + (y + 4 - dy) % 4
            arrived(cf.at[q, chunk_rows(source)], gr.at[q, slot])
        for slot in range(8):
            arrived(ein.at[q, chunk_rows(slot)], er.at[q, slot])

    products(0)
    x_pass_on(0)
    products(1)
    normed_forward()
    z_send(0)
    x_pass_on(1)
    normed_ready()
    couple(0)
    z_send(1)
    couple(1)
    z_share(0)
    z_share(1)
    gather(0)
    columns_out(0)
    gather(1)
    columns_out(1)
    finished(0)
    finished(1)
    block = jnp.concatenate([cf[0, mine_rows, :], cf[1, mine_rows, :]], 1)
    s_out[mine_rows, :] = 0.5 * (block + block.T)
    mirrored = jnp.concatenate([ein[0].T, ein[1].T], 0)
    s_out[other_rows, :] = 0.5 * (jnp.concatenate([cf[0, other_rows, :], cf[1, other_rows, :]], 1) + mirrored)
    for copy, mine in first:

        @pl.when(jnp.logical_not(mine))
        def _():
            copy.wait_send()

    @pl.when(crosses)
    def _():
        for q in range(2):
            for copy in cross_copies(q):
                copy.wait_send()

    for copy in sent:
        copy.wait_send()


def body(ancestor_inverse, tile_structure, factor, factor_normalizer, pivot_inverse):
    tile, width = factor.shape
    part = width // 4
    rows, columns = ancestor_inverse.shape
    chunk = width // 16
    vmem, dma = pltpu.VMEM, pltpu.SemaphoreType.DMA
    anywhere = pl.BlockSpec(memory_space=pltpu.HBM)
    in_vmem = pl.BlockSpec(memory_space=pltpu.VMEM)
    ancestor_columns, symmetric = pl.pallas_call(
        kernel,
        out_shape=(
            jax.ShapeDtypeStruct((tile, 2 * part), F32),
            jax.ShapeDtypeStruct((width, 2 * part), F32),
        ),
        in_specs=[in_vmem, anywhere, anywhere, anywhere],
        out_specs=(in_vmem, in_vmem),
        scratch_shapes=[
            vmem((rows, columns), F32),
            vmem((rows, columns), BF16),
            vmem((rows, columns), BF16),
            vmem((tile, width), F32),
            vmem((4, width, part), F32),
            vmem((2, tile, part), F32),
            vmem((width, 4 * tile), BF16),
            vmem((width, 4 * tile), BF16),
            vmem((2, 8, 4, tile // 4, part), F32),
            vmem((2, columns, 2 * part), BF16),
            vmem((2, rows, part), F32),
            vmem((2, 2, 2 * tile, part), F32),
            vmem((2, 2, 4 * tile, part), F32),
            vmem((2, 4 * tile, part), F32),
            vmem((2, 3, tile, part), F32),
            vmem((2, tile, part), F32),
            vmem((2, width, part), F32),
            vmem((2, 15, chunk, part), F32),
            vmem((2, chunk, part), F32),
            vmem((2, 8, chunk, part), F32),
            vmem((2, width, part), F32),
            vmem((2, 2 * part, part), F32),
            vmem((2, 8, tile // 4, part), F32),
            vmem((4, 4, tile, part), F32),
            dma((16,)),
            dma((5,)),
            dma((2, 7)),
            dma((2, 8)),
            dma((3,)),
            dma((4,)),
            dma((3,)),
            dma((4,)),
            dma((2, 8)),
            dma((2, 8)),
            dma((2, 6)),
            dma((2, 6)),
            dma((2, 6)),
            dma((2, 6)),
            dma((2, 3)),
            dma((2, 3)),
            dma((2, 15)),
            dma((2, 15)),
            dma((2, 7)),
            dma((2, 8)),
            dma((2, 15)),
            dma((2, 15)),
            dma((2, 16)),
            dma((2, 8)),
        ],
        compiler_params=pltpu.CompilerParams(collective_id=0, has_side_effects=True, vmem_limit_bytes=40 * 1024 * 1024),
    )(
        tile_structure.astype(F32),
        *(pltpu.with_memory_space_constraint(value, pltpu.HBM) for value in (ancestor_inverse, factor, factor_normalizer)),
    )
    return ancestor_columns, pivot_inverse - symmetric


def solution(mesh):
    return jax.shard_map(
        body,
        mesh=mesh,
        in_specs=(P("row", "col"), P("row", "col"), P(("row", "col"), None), P(), P(None, "rep")),
        out_specs=(P(("row", "col"), "rep"), P(None, "rep")),
        check_vma=False,
    )
```

```python
import jax
import jax.numpy as jnp
from jax import lax
from jax.experimental import pallas as pl
from jax.experimental.pallas import tpu as pltpu
from jax.sharding import PartitionSpec as P

F32 = jnp.float32
BF16 = jnp.bfloat16
MESH = pl.DeviceIdType.MESH


def split(value):
    high = value.astype(BF16)
    return high, (value - high.astype(F32)).astype(BF16)


def dot(left, right):
    return jnp.dot(left, right, preferred_element_type=F32)


def dot3(left, right):
    lh, ll = left
    rh, rl = right
    return dot(lh, rh) + (dot(lh, rl) + dot(ll, rh))


def kernel(
    tiles, a_hbm, f_hbm, n_hbm, y_out, s_out,
    af, ah, al, fac, nrm, nown, nth, ntl, xf, xc, p, gin, rin, zc, zin, yb, cp, win, tv, uin, cf, ein,
    bn, nz, a_sem, i_sem, bs, br, ns, nr, ms, mr, s1s, s1r, ys, yr, xs, xr, zs, zr, ws, wr, us, ur, gs, gr, es, er,
):
    row, col, rep = (lax.axis_index(name) for name in ("row", "col", "rep"))
    tile, width = fac.shape
    half = width // 2
    part = half // 2
    quad = 4 * tile
    chunk = width // 16
    x, z_lo, z_hi, y = col // 4, col % 4, row // 4, row % 4
    z = z_hi * 4 + z_lo
    sent = []

    def place(px, py, pz):
        return (pz // 4 * 4 + py, px * 4 + pz % 4, rep)

    def send(src, dst, send_sem, recv_sem, device):
        copy = pltpu.make_async_remote_copy(
            src_ref=src, dst_ref=dst, send_sem=send_sem, recv_sem=recv_sem,
            device_id=device, device_id_type=MESH,
        )
        copy.start()
        sent.append(copy)

    def arrived(dst, sem):
        pltpu.make_async_copy(dst, dst, sem).wait()

    load_f = pltpu.make_async_copy(f_hbm, fac, i_sem.at[0])
    load_f.start()
    slices = [rep * 2, rep * 2 + 1, 2 - rep * 2, 3 - rep * 2]

    def slice_of(index):
        return pl.ds(pl.multiple_of(slices[index] * part, part), part)

    load_n = [pltpu.make_async_copy(n_hbm.at[:, slice_of(i)], nrm.at[i], i_sem.at[1 + i]) for i in range(4)]
    for load in load_n:
        load.start()

    def rows_of(a):
        return pl.ds(pl.multiple_of(a * tile, tile), tile)

    for a in range(16):
        pltpu.make_async_copy(a_hbm.at[rows_of(a)], af.at[rows_of(a)], a_sem.at[a]).start()

    barrier = pltpu.get_barrier_semaphore()
    for dx in range(4):
        for dy in range(4):
            near = place((x + dx) % 4, (y + dy) % 4, z)
            if dx or dy:
                pl.semaphore_signal(barrier, inc=1, device_id=near, device_id_type=MESH)
            pl.semaphore_signal(barrier, inc=1, device_id=(near[0], near[1], 1 - rep), device_id_type=MESH)
    for dz in range(1, 8):
        pl.semaphore_signal(barrier, inc=1, device_id=place(x, y, (z + dz) % 8), device_id_type=MESH)
    for slot in range(8):
        from_row, from_col = row, col % 2 * 8 + slot
        mine = jnp.logical_and(from_row == row, from_col == col)

        @pl.when(jnp.logical_not(mine))
        def _():
            pl.semaphore_signal(barrier, inc=1, device_id=(from_row, from_col, rep), device_id_type=MESH)

    load_f.wait()

    def normed(index):
        load_n[index].wait()
        value = dot3(split(fac[...]), split(nrm[index]))
        if index < 2:
            nown[index] = value
        return value

    def keep_transposed(index, value):
        high, low = split(value.T)
        nth[slice_of(index), rows_of(z_lo)] = high
        ntl[slice_of(index), rows_of(z_lo)] = low

    own_slices = pl.ds(rep * 2, 2)

    def normed_share():
        for dz in (2, 1, 3):
            to = place(x, y, z_hi * 4 + (z_lo + dz) % 4)
            send(nown, nz.at[z_lo, own_slices], ns.at[dz - 1], nr.at[z_lo], to)

    def normed_forward():
        for dz in range(1, 4):
            peer = (z_lo + dz) % 4
            arrived(nz.at[peer, own_slices], nr.at[peer])
            send(nz.at[peer, own_slices], nz.at[peer, own_slices], ms.at[dz - 1], mr.at[peer], (row, col, 1 - rep))

    def normed_ready():
        for dz in range(1, 4):
            peer = (z_lo + dz) % 4
            arrived(nz.at[peer, pl.ds(2 - rep * 2, 2)], mr.at[peer])
            for index in range(4):
                high, low = split(nz[peer, index].T)
                nth[index * part : (index + 1) * part, rows_of(peer)] = high
                ntl[index * part : (index + 1) * part, rows_of(peer)] = low

    value = normed(0)

    kth = col % 8
    to_col = 2 * row + col // 8
    for ty in range(1, 4):
        to = place(x, (y + ty) % 4, (z + 4) % 8)
        pl.semaphore_signal(barrier, inc=1, device_id=to, device_id_type=MESH)
    pl.semaphore_wait(barrier, 31 + 7 + 3 + 8 - (col % 2 == col // 8).astype(jnp.int32))
    piece_rows = tile // 4
    first = []

    def row_send(q):
        for zh in range(2):
            for ty in range(4):
                if zh or ty:
                    to_y, to_z = (y + ty) % 4, (z + zh * 4) % 8
                    source = nown.at[q, pl.ds(pl.multiple_of(to_y * piece_rows, piece_rows), piece_rows)]
                    send(source, bn.at[q, row], bs.at[q, zh * 4 + ty - 1], br.at[q, row], place(x, to_y, to_z))
        bn[q, row] = nown[q, pl.ds(pl.multiple_of(y * piece_rows, piece_rows), piece_rows)]

    def plane_send(q):
        for shift in range(8):
            owner = (col // 2 + shift) % 8

            @pl.when(owner != row)
            def _():
                arrived(bn.at[q, owner], br.at[q, owner])

            target = 2 * owner + col // 8
            mine = target == col
            copy = pltpu.make_async_remote_copy(
                src_ref=bn.at[q, owner], dst_ref=xf.at[q, kth, y], send_sem=s1s.at[q, shift], recv_sem=s1r.at[q, kth],
                device_id=(row, target, rep), device_id_type=MESH,
            )
            first.append((copy, mine))

            @pl.when(jnp.logical_not(mine))
            def _():
                copy.start()

            @pl.when(mine)
            def _():
                pltpu.make_async_copy(bn.at[q, owner], xf.at[q, kth, y], s1r.at[q, kth]).start()

    def mask_rows(a, carry):
        pltpu.make_async_copy(a_hbm.at[rows_of(a)], af.at[rows_of(a)], a_sem.at[a]).wait()
        marks = tiles[pl.ds(a, 1), :]
        for b in range(8):
            columns = slice(b * tile, (b + 1) * tile)
            high, low = split(af[rows_of(a), columns] * marks[:, b : b + 1])
            ah[rows_of(a), columns] = high
            al[rows_of(a), columns] = low
        return carry

    def y_exchange(q):
        for group in range(2):
            four = pl.ds(group * 4, 4)
            for slot in range(4):
                arrived(xf.at[q, group * 4 + slot, y], s1r.at[q, group * 4 + slot])
            for dy in (1, 3, 2):
                index = group * 3 + dy - 1
                send(xf.at[q, four, y], xf.at[q, four, y], ys.at[q, index], yr.at[q, index], place(x, (y + dy) % 4, z))

    row_send(0)
    keep_transposed(0, value)
    for index in range(1, 4):
        keep_transposed(index, normed(index))
    lax.fori_loop(0, 2, mask_rows, 0)
    row_send(1)
    lax.fori_loop(2, 7, mask_rows, 0)
    plane_send(0)
    lax.fori_loop(7, 13, mask_rows, 0)
    plane_send(1)
    y_exchange(0)
    lax.fori_loop(13, 16, mask_rows, 0)
    y_exchange(1)
    normed_share()

    def x_ready(q):
        for dy in range(1, 4):
            for group in range(2):
                arrived(xf.at[q, pl.ds(group * 4, 4), (y + 4 - dy) % 4], yr.at[q, group * 3 + dy - 1])
        high, low = split(xf[q].reshape(8 * tile, part))
        xc[q, :, :part] = high
        xc[q, :, part:] = low

    xp, xo, xm = (x + 1) % 4, (x + 2) % 4, (x + 3) % 4

    def piece(block, side):
        return pl.ds(pl.multiple_of(block * quad + side * 2 * tile, 2 * tile), 2 * tile)

    sides = [slice(0, 2 * tile), slice(2 * tile, quad)]

    def product(q, block, side):
        rows = piece(block, side)
        both = dot(ah[rows, :], xc[q])
        p[q, rows, :] = both[:, :part] + (both[:, part:] + dot(al[rows, :], xc[q, :, :part]))

    def x_send(q, index, block, side, target, dst):
        send(p.at[q, piece(block, side)], dst, xs.at[q, index], xr.at[q, index], place(target, y, z))

    def products(q):
        x_ready(q)
        product(q, xo, 0)
        x_send(q, 0, xo, 0, xp, gin.at[q, 0])
        product(q, xo, 1)
        x_send(q, 1, xo, 1, xm, gin.at[q, 1])
        product(q, xp, 1)
        x_send(q, 2, xp, 1, xp, rin.at[q, 0, sides[1]])
        product(q, xm, 0)
        x_send(q, 3, xm, 0, xm, rin.at[q, 1, sides[0]])
        product(q, xp, 0)
        product(q, xm, 1)
        product(q, x, 0)
        product(q, x, 1)

    def x_pass_on(q):
        arrived(gin.at[q, 0], xr.at[q, 0])
        p[q, piece(xp, 0), :] += gin[q, 0]
        x_send(q, 4, xp, 0, xp, rin.at[q, 0, sides[0]])
        arrived(gin.at[q, 1], xr.at[q, 1])
        p[q, piece(xm, 1), :] += gin[q, 1]
        x_send(q, 5, xm, 1, xm, rin.at[q, 1, sides[1]])

    def x_sum(q):
        arrived(rin.at[q, 0, sides[1]], xr.at[q, 2])
        arrived(rin.at[q, 1, sides[0]], xr.at[q, 3])
        arrived(rin.at[q, 0, sides[0]], xr.at[q, 4])
        arrived(rin.at[q, 1, sides[1]], xr.at[q, 5])
        for side in range(2):
            zc[q, sides[side]] = p[q, piece(x, side), :] + (rin[q, 0, sides[side]] + rin[q, 1, sides[side]])

    def z_send(q):
        for dz in (2, 1, 3):
            to = (z_lo + dz) % 4
            send(zc.at[q, rows_of(to)], zin.at[q, dz - 1], zs.at[q, dz - 1], zr.at[q, dz - 1], place(x, y, z_hi * 4 + to))

    def plane():
        return [(dx, dy, dx * 4 + dy - 1) for dx in (2, 1, 3, 0) for dy in (2, 1, 3, 0) if dx or dy]

    def chunk_rows(index):
        return pl.ds(pl.multiple_of(index * chunk, chunk), chunk)

    def couple(q):
        sums = split(-zc[q])
        for dx in (2, 1, 3, 0):
            tx = (x + dx) % 4
            rows = pl.ds(pl.multiple_of(tx * 4 * chunk, 4 * chunk), 4 * chunk)
            cp[q, rows, :] = dot3((nth[rows, :], ntl[rows, :]), sums)
            for dy in (2, 1, 3, 0):
                if dx or dy:
                    ty, slot = (y + dy) % 4, dx * 4 + dy - 1
                    source = cp.at[q, chunk_rows(tx * 4 + ty)]
                    send(source, win.at[q, slot], ws.at[q, slot], wr.at[q, slot], place(tx, ty, z))

    def columns_out(q):
        total = zc[q, rows_of(z_lo), :]
        for dz in range(1, 4):
            arrived(zin.at[q, dz - 1], zr.at[q, dz - 1])
            total += zin[q, dz - 1]
        y_out[:, q * part : (q + 1) * part] = -total

    own = x * 4 + y

    def z_share(q):
        total = cp[q, chunk_rows(own), :]
        for _, _, slot in plane():
            arrived(win.at[q, slot], wr.at[q, slot])
            total += win[q, slot]
        uin[q, z] = total
        tv[q] = total
        for dz in (4, 3, 5, 2, 6, 1, 7):
            send(tv.at[q], uin.at[q, z], us.at[q, dz - 1], ur.at[q, z], place(x, y, (z + dz) % 8))

    def gather(q):
        for dz in range(1, 8):
            source = (z + dz) % 8
            arrived(uin.at[q, source], ur.at[q, source])
        total = uin[q, 0]
        for source in range(1, 8):
            total += uin[q, source]
        cf[q, chunk_rows(own), :] = total
        for dx, dy, slot in plane():
            to = place((x + dx) % 4, (y + dy) % 4, z)
            send(cf.at[q, chunk_rows(own)], cf.at[q, chunk_rows(own)], gs.at[q, slot], gr.at[q, slot], to)

        @pl.when(crosses)
        def _():
            for copy in cross_copies(q):
                copy.start()

    crosses = own // 8 != rep

    def cross_copies(q):
        copies = []
        for dx in (2, 1, 3, 0):
            for dy in (2, 1, 3, 0):
                to = place((x + dx) % 4, (y + dy) % 4, z)
                copies.append(
                    pltpu.make_async_remote_copy(
                        src_ref=cf.at[q, chunk_rows(own)], dst_ref=ein.at[q, chunk_rows(own % 8)],
                        send_sem=es.at[q, dx * 4 + dy], recv_sem=er.at[q, own % 8],
                        device_id=(to[0], to[1], 1 - rep), device_id_type=MESH,
                    )
                )
        return copies

    mine_rows = pl.ds(pl.multiple_of(rep * half, half), half)
    other_rows = pl.ds(pl.multiple_of((1 - rep) * half, half), half)

    def finished(q):
        for dx, dy, slot in plane():
            source = (x + 4 - dx) % 4 * 4 + (y + 4 - dy) % 4
            arrived(cf.at[q, chunk_rows(source)], gr.at[q, slot])
        for slot in range(8):
            arrived(ein.at[q, chunk_rows(slot)], er.at[q, slot])

    products(0)
    x_pass_on(0)
    products(1)
    normed_forward()
    x_sum(0)
    z_send(0)
    x_pass_on(1)
    normed_ready()
    couple(0)
    x_sum(1)
    couple(1)
    z_share(0)
    z_share(1)
    z_send(1)
    gather(0)
    gather(1)
    columns_out(0)
    columns_out(1)
    finished(0)
    finished(1)
    block = jnp.concatenate([cf[0, mine_rows, :], cf[1, mine_rows, :]], 1)
    s_out[mine_rows, :] = 0.5 * (block + block.T)
    mirrored = jnp.concatenate([ein[0].T, ein[1].T], 0)
    s_out[other_rows, :] = 0.5 * (jnp.concatenate([cf[0, other_rows, :], cf[1, other_rows, :]], 1) + mirrored)
    for copy, mine in first:

        @pl.when(jnp.logical_not(mine))
        def _():
            copy.wait_send()

    @pl.when(crosses)
    def _():
        for q in range(2):
            for copy in cross_copies(q):
                copy.wait_send()

    for copy in sent:
        copy.wait_send()


def body(ancestor_inverse, tile_structure, factor, factor_normalizer, pivot_inverse):
    tile, width = factor.shape
    part = width // 4
    rows, columns = ancestor_inverse.shape
    chunk = width // 16
    vmem, dma = pltpu.VMEM, pltpu.SemaphoreType.DMA
    anywhere = pl.BlockSpec(memory_space=pltpu.HBM)
    in_vmem = pl.BlockSpec(memory_space=pltpu.VMEM)
    ancestor_columns, symmetric = pl.pallas_call(
        kernel,
        out_shape=(
            jax.ShapeDtypeStruct((tile, 2 * part), F32),
            jax.ShapeDtypeStruct((width, 2 * part), F32),
        ),
        in_specs=[in_vmem, anywhere, anywhere, anywhere],
        out_specs=(in_vmem, in_vmem),
        scratch_shapes=[
            vmem((rows, columns), F32),
            vmem((rows, columns), BF16),
            vmem((rows, columns), BF16),
            vmem((tile, width), F32),
            vmem((4, width, part), F32),
            vmem((2, tile, part), F32),
            vmem((width, 4 * tile), BF16),
            vmem((width, 4 * tile), BF16),
            vmem((2, 8, 4, tile // 4, part), F32),
            vmem((2, columns, 2 * part), BF16),
            vmem((2, rows, part), F32),
            vmem((2, 2, 2 * tile, part), F32),
            vmem((2, 2, 4 * tile, part), F32),
            vmem((2, 4 * tile, part), F32),
            vmem((2, 3, tile, part), F32),
            vmem((2, tile, part), F32),
            vmem((2, width, part), F32),
            vmem((2, 15, chunk, part), F32),
            vmem((2, chunk, part), F32),
            vmem((2, 8, chunk, part), F32),
            vmem((2, width, part), F32),
            vmem((2, 2 * part, part), F32),
            vmem((2, 8, tile // 4, part), F32),
            vmem((4, 4, tile, part), F32),
            dma((16,)),
            dma((5,)),
            dma((2, 7)),
            dma((2, 8)),
            dma((3,)),
            dma((4,)),
            dma((3,)),
            dma((4,)),
            dma((2, 8)),
            dma((2, 8)),
            dma((2, 6)),
            dma((2, 6)),
            dma((2, 6)),
            dma((2, 6)),
            dma((2, 3)),
            dma((2, 3)),
            dma((2, 15)),
            dma((2, 15)),
            dma((2, 7)),
            dma((2, 8)),
            dma((2, 15)),
            dma((2, 15)),
            dma((2, 16)),
            dma((2, 8)),
        ],
        compiler_params=pltpu.CompilerParams(collective_id=0, has_side_effects=True, vmem_limit_bytes=40 * 1024 * 1024),
    )(
        tile_structure.astype(F32),
        *(pltpu.with_memory_space_constraint(value, pltpu.HBM) for value in (ancestor_inverse, factor, factor_normalizer)),
    )
    return ancestor_columns, pivot_inverse - symmetric


def solution(mesh):
    return jax.shard_map(
        body,
        mesh=mesh,
        in_specs=(P("row", "col"), P("row", "col"), P(("row", "col"), None), P(), P(None, "rep")),
        out_specs=(P(("row", "col"), "rep"), P(None, "rep")),
        check_vma=False,
    )
```

```python
import jax
import jax.numpy as jnp
from jax import lax
from jax.experimental import pallas as pl
from jax.experimental.pallas import tpu as pltpu
from jax.sharding import PartitionSpec as P

F32 = jnp.float32
BF16 = jnp.bfloat16
MESH = pl.DeviceIdType.MESH


def split(value):
    high = value.astype(BF16)
    return high, (value - high.astype(F32)).astype(BF16)


def dot(left, right):
    return jnp.dot(left, right, preferred_element_type=F32)


def dot3(left, right):
    lh, ll = left
    rh, rl = right
    return dot(lh, rh) + (dot(lh, rl) + dot(ll, rh))


def kernel(
    tiles, a_hbm, f_hbm, n_hbm, y_out, s_out,
    af, ah, al, fac, nrm, nown, nth, ntl, xf, xc, p, gin, rin, zc, zin, yb, cp, win, tv, uin, cf, ein,
    bn, nz, a_sem, i_sem, bs, br, ns, nr, ms, mr, s1s, s1r, ys, yr, xs, xr, zs, zr, ws, wr, us, ur, gs, gr, es, er,
):
    row, col, rep = (lax.axis_index(name) for name in ("row", "col", "rep"))
    tile, width = fac.shape
    half = width // 2
    part = half // 2
    quad = 4 * tile
    chunk = width // 16
    x, z_lo, z_hi, y = col // 4, col % 4, row // 4, row % 4
    z = z_hi * 4 + z_lo
    sent = []

    def place(px, py, pz):
        return (pz // 4 * 4 + py, px * 4 + pz % 4, rep)

    def send(src, dst, send_sem, recv_sem, device):
        copy = pltpu.make_async_remote_copy(
            src_ref=src, dst_ref=dst, send_sem=send_sem, recv_sem=recv_sem,
            device_id=device, device_id_type=MESH,
        )
        copy.start()
        sent.append(copy)

    def arrived(dst, sem):
        pltpu.make_async_copy(dst, dst, sem).wait()

    load_f = pltpu.make_async_copy(f_hbm, fac, i_sem.at[0])
    load_f.start()
    slices = [rep * 2, rep * 2 + 1, 2 - rep * 2, 3 - rep * 2]

    def slice_of(index):
        return pl.ds(pl.multiple_of(slices[index] * part, part), part)

    load_n = [pltpu.make_async_copy(n_hbm.at[:, slice_of(i)], nrm.at[i], i_sem.at[1 + i]) for i in range(4)]
    for load in load_n:
        load.start()

    def rows_of(a):
        return pl.ds(pl.multiple_of(a * tile, tile), tile)

    for a in range(16):
        pltpu.make_async_copy(a_hbm.at[rows_of(a)], af.at[rows_of(a)], a_sem.at[a]).start()

    barrier = pltpu.get_barrier_semaphore()
    for dx in range(4):
        for dy in range(4):
            near = place((x + dx) % 4, (y + dy) % 4, z)
            if dx or dy:
                pl.semaphore_signal(barrier, inc=1, device_id=near, device_id_type=MESH)
            pl.semaphore_signal(barrier, inc=1, device_id=(near[0], near[1], 1 - rep), device_id_type=MESH)
    for dz in range(1, 8):
        pl.semaphore_signal(barrier, inc=1, device_id=place(x, y, (z + dz) % 8), device_id_type=MESH)
    for slot in range(8):
        from_row, from_col = row, col % 2 * 8 + slot
        mine = jnp.logical_and(from_row == row, from_col == col)

        @pl.when(jnp.logical_not(mine))
        def _():
            pl.semaphore_signal(barrier, inc=1, device_id=(from_row, from_col, rep), device_id_type=MESH)

    load_f.wait()

    def normed(index):
        load_n[index].wait()
        value = dot3(split(fac[...]), split(nrm[index]))
        if index < 2:
            nown[index] = value
        return value

    def keep_transposed(index, value):
        high, low = split(value.T)
        nth[slice_of(index), rows_of(z_lo)] = high
        ntl[slice_of(index), rows_of(z_lo)] = low

    own_slices = pl.ds(rep * 2, 2)

    def normed_share():
        for dz in (2, 1, 3):
            to = place(x, y, z_hi * 4 + (z_lo + dz) % 4)
            send(nown, nz.at[z_lo, own_slices], ns.at[dz - 1], nr.at[z_lo], to)

    def normed_forward():
        for dz in range(1, 4):
            peer = (z_lo + dz) % 4
            arrived(nz.at[peer, own_slices], nr.at[peer])
            send(nz.at[peer, own_slices], nz.at[peer, own_slices], ms.at[dz - 1], mr.at[peer], (row, col, 1 - rep))

    def normed_ready():
        for dz in range(1, 4):
            peer = (z_lo + dz) % 4
            arrived(nz.at[peer, pl.ds(2 - rep * 2, 2)], mr.at[peer])
            for index in range(4):
                high, low = split(nz[peer, index].T)
                nth[index * part : (index + 1) * part, rows_of(peer)] = high
                ntl[index * part : (index + 1) * part, rows_of(peer)] = low

    value = normed(0)

    kth = col % 8
    to_col = 2 * row + col // 8
    for ty in range(1, 4):
        to = place(x, (y + ty) % 4, (z + 4) % 8)
        pl.semaphore_signal(barrier, inc=1, device_id=to, device_id_type=MESH)
    pl.semaphore_wait(barrier, 31 + 7 + 3 + 8 - (col % 2 == col // 8).astype(jnp.int32))
    piece_rows = tile // 4
    first = []

    def row_send(q):
        for zh in range(2):
            for ty in range(4):
                if zh or ty:
                    to_y, to_z = (y + ty) % 4, (z + zh * 4) % 8
                    source = nown.at[q, pl.ds(pl.multiple_of(to_y * piece_rows, piece_rows), piece_rows)]
                    send(source, bn.at[q, row], bs.at[q, zh * 4 + ty - 1], br.at[q, row], place(x, to_y, to_z))
        bn[q, row] = nown[q, pl.ds(pl.multiple_of(y * piece_rows, piece_rows), piece_rows)]

    def plane_send(q):
        for shift in range(8):
            owner = (col // 2 + shift) % 8

            @pl.when(owner != row)
            def _():
                arrived(bn.at[q, owner], br.at[q, owner])

            target = 2 * owner + col // 8
            mine = target == col
            copy = pltpu.make_async_remote_copy(
                src_ref=bn.at[q, owner], dst_ref=xf.at[q, kth, y], send_sem=s1s.at[q, shift], recv_sem=s1r.at[q, kth],
                device_id=(row, target, rep), device_id_type=MESH,
            )
            first.append((copy, mine))

            @pl.when(jnp.logical_not(mine))
            def _():
                copy.start()

            @pl.when(mine)
            def _():
                pltpu.make_async_copy(bn.at[q, owner], xf.at[q, kth, y], s1r.at[q, kth]).start()

    def mask_rows(a, carry):
        pltpu.make_async_copy(a_hbm.at[rows_of(a)], af.at[rows_of(a)], a_sem.at[a]).wait()
        marks = tiles[pl.ds(a, 1), :]
        for b in range(8):
            columns = slice(b * tile, (b + 1) * tile)
            high, low = split(af[rows_of(a), columns] * marks[:, b : b + 1])
            ah[rows_of(a), columns] = high
            al[rows_of(a), columns] = low
        return carry

    def y_exchange(q):
        for group in range(2):
            four = pl.ds(group * 4, 4)
            for slot in range(4):
                arrived(xf.at[q, group * 4 + slot, y], s1r.at[q, group * 4 + slot])
            for dy in (1, 3, 2):
                index = group * 3 + dy - 1
                send(xf.at[q, four, y], xf.at[q, four, y], ys.at[q, index], yr.at[q, index], place(x, (y + dy) % 4, z))

    row_send(0)
    keep_transposed(0, value)
    for index in range(1, 4):
        keep_transposed(index, normed(index))
    lax.fori_loop(0, 2, mask_rows, 0)
    row_send(1)
    lax.fori_loop(2, 7, mask_rows, 0)
    plane_send(0)
    lax.fori_loop(7, 13, mask_rows, 0)
    plane_send(1)
    y_exchange(0)
    lax.fori_loop(13, 16, mask_rows, 0)
    y_exchange(1)
    normed_share()

    def x_ready(q):
        for dy in range(1, 4):
            for group in range(2):
                arrived(xf.at[q, pl.ds(group * 4, 4), (y + 4 - dy) % 4], yr.at[q, group * 3 + dy - 1])
        high, low = split(xf[q].reshape(8 * tile, part))
        xc[q, :, :part] = high
        xc[q, :, part:] = low

    xp, xo, xm = (x + 1) % 4, (x + 2) % 4, (x + 3) % 4

    def piece(block, side):
        return pl.ds(pl.multiple_of(block * quad + side * 2 * tile, 2 * tile), 2 * tile)

    sides = [slice(0, 2 * tile), slice(2 * tile, quad)]

    def product(q, block, side):
        rows = piece(block, side)
        both = dot(ah[rows, :], xc[q])
        p[q, rows, :] = both[:, :part] + (both[:, part:] + dot(al[rows, :], xc[q, :, :part]))

    def x_send(q, index, block, side, target, dst):
        send(p.at[q, piece(block, side)], dst, xs.at[q, index], xr.at[q, index], place(target, y, z))

    def products(q):
        x_ready(q)
        product(q, xo, 0)
        x_send(q, 0, xo, 0, xp, gin.at[q, 0])
        product(q, xo, 1)
        x_send(q, 1, xo, 1, xm, gin.at[q, 1])
        product(q, xp, 1)
        x_send(q, 2, xp, 1, xp, rin.at[q, 0, sides[1]])
        product(q, xm, 0)
        x_send(q, 3, xm, 0, xm, rin.at[q, 1, sides[0]])
        product(q, xp, 0)
        product(q, xm, 1)
        product(q, x, 0)
        product(q, x, 1)

    def x_pass_on(q):
        arrived(gin.at[q, 0], xr.at[q, 0])
        p[q, piece(xp, 0), :] += gin[q, 0]
        x_send(q, 4, xp, 0, xp, rin.at[q, 0, sides[0]])
        arrived(gin.at[q, 1], xr.at[q, 1])
        p[q, piece(xm, 1), :] += gin[q, 1]
        x_send(q, 5, xm, 1, xm, rin.at[q, 1, sides[1]])

    def x_sum(q):
        arrived(rin.at[q, 0, sides[1]], xr.at[q, 2])
        arrived(rin.at[q, 1, sides[0]], xr.at[q, 3])
        arrived(rin.at[q, 0, sides[0]], xr.at[q, 4])
        arrived(rin.at[q, 1, sides[1]], xr.at[q, 5])
        for side in range(2):
            zc[q, sides[side]] = p[q, piece(x, side), :] + (rin[q, 0, sides[side]] + rin[q, 1, sides[side]])

    def z_send(q):
        for dz in (2, 1, 3):
            to = (z_lo + dz) % 4
            send(zc.at[q, rows_of(to)], zin.at[q, dz - 1], zs.at[q, dz - 1], zr.at[q, dz - 1], place(x, y, z_hi * 4 + to))

    def plane():
        return [(dx, dy, dx * 4 + dy - 1) for dx in (2, 1, 3, 0) for dy in (2, 1, 3, 0) if dx or dy]

    def chunk_rows(index):
        return pl.ds(pl.multiple_of(index * chunk, chunk), chunk)

    def couple(q):
        sums = split(-zc[q])
        for dx in (2, 1, 3, 0):
            tx = (x + dx) % 4
            rows = pl.ds(pl.multiple_of(tx * 4 * chunk, 4 * chunk), 4 * chunk)
            cp[q, rows, :] = dot3((nth[rows, :], ntl[rows, :]), sums)
            for dy in (2, 1, 3, 0):
                if dx or dy:
                    ty, slot = (y + dy) % 4, dx * 4 + dy - 1
                    source = cp.at[q, chunk_rows(tx * 4 + ty)]
                    send(source, win.at[q, slot], ws.at[q, slot], wr.at[q, slot], place(tx, ty, z))

    def columns_out(q):
        total = zc[q, rows_of(z_lo), :]
        for dz in range(1, 4):
            arrived(zin.at[q, dz - 1], zr.at[q, dz - 1])
            total += zin[q, dz - 1]
        y_out[:, q * part : (q + 1) * part] = -total

    own = x * 4 + y

    def z_share(q):
        total = cp[q, chunk_rows(own), :]
        for _, _, slot in plane():
            arrived(win.at[q, slot], wr.at[q, slot])
            total += win[q, slot]
        uin[q, z] = total
        tv[q] = total
        for dz in (4, 3, 5, 2, 6, 1, 7):
            send(tv.at[q], uin.at[q, z], us.at[q, dz - 1], ur.at[q, z], place(x, y, (z + dz) % 8))

    def gather(q):
        for dz in range(1, 8):
            source = (z + dz) % 8
            arrived(uin.at[q, source], ur.at[q, source])
        total = uin[q, 0]
        for source in range(1, 8):
            total += uin[q, source]
        cf[q, chunk_rows(own), :] = total
        for dx, dy, slot in plane():
            to = place((x + dx) % 4, (y + dy) % 4, z)
            send(cf.at[q, chunk_rows(own)], cf.at[q, chunk_rows(own)], gs.at[q, slot], gr.at[q, slot], to)

        @pl.when(crosses)
        def _():
            for copy in cross_copies(q):
                copy.start()

    crosses = own // 8 != rep

    def cross_copies(q):
        copies = []
        for dx in (2, 1, 3, 0):
            for dy in (2, 1, 3, 0):
                to = place((x + dx) % 4, (y + dy) % 4, z)
                copies.append(
                    pltpu.make_async_remote_copy(
                        src_ref=cf.at[q, chunk_rows(own)], dst_ref=ein.at[q, chunk_rows(own % 8)],
                        send_sem=es.at[q, dx * 4 + dy], recv_sem=er.at[q, own % 8],
                        device_id=(to[0], to[1], 1 - rep), device_id_type=MESH,
                    )
                )
        return copies

    mine_rows = pl.ds(pl.multiple_of(rep * half, half), half)
    other_rows = pl.ds(pl.multiple_of((1 - rep) * half, half), half)

    def finished(q):
        for dx, dy, slot in plane():
            source = (x + 4 - dx) % 4 * 4 + (y + 4 - dy) % 4
            arrived(cf.at[q, chunk_rows(source)], gr.at[q, slot])
        for slot in range(8):
            arrived(ein.at[q, chunk_rows(slot)], er.at[q, slot])

    products(0)
    x_pass_on(0)
    products(1)
    normed_forward()
    x_sum(0)
    z_send(0)
    x_pass_on(1)
    normed_ready()
    couple(0)
    x_sum(1)
    couple(1)
    z_share(0)
    z_share(1)
    gather(0)
    z_send(1)
    gather(1)
    columns_out(0)
    columns_out(1)
    finished(0)
    finished(1)
    block = jnp.concatenate([cf[0, mine_rows, :], cf[1, mine_rows, :]], 1)
    s_out[mine_rows, :] = 0.5 * (block + block.T)
    mirrored = jnp.concatenate([ein[0].T, ein[1].T], 0)
    s_out[other_rows, :] = 0.5 * (jnp.concatenate([cf[0, other_rows, :], cf[1, other_rows, :]], 1) + mirrored)
    for copy, mine in first:

        @pl.when(jnp.logical_not(mine))
        def _():
            copy.wait_send()

    @pl.when(crosses)
    def _():
        for q in range(2):
            for copy in cross_copies(q):
                copy.wait_send()

    for copy in sent:
        copy.wait_send()


def body(ancestor_inverse, tile_structure, factor, factor_normalizer, pivot_inverse):
    tile, width = factor.shape
    part = width // 4
    rows, columns = ancestor_inverse.shape
    chunk = width // 16
    vmem, dma = pltpu.VMEM, pltpu.SemaphoreType.DMA
    anywhere = pl.BlockSpec(memory_space=pltpu.HBM)
    in_vmem = pl.BlockSpec(memory_space=pltpu.VMEM)
    ancestor_columns, symmetric = pl.pallas_call(
        kernel,
        out_shape=(
            jax.ShapeDtypeStruct((tile, 2 * part), F32),
            jax.ShapeDtypeStruct((width, 2 * part), F32),
        ),
        in_specs=[in_vmem, anywhere, anywhere, anywhere],
        out_specs=(in_vmem, in_vmem),
        scratch_shapes=[
            vmem((rows, columns), F32),
            vmem((rows, columns), BF16),
            vmem((rows, columns), BF16),
            vmem((tile, width), F32),
            vmem((4, width, part), F32),
            vmem((2, tile, part), F32),
            vmem((width, 4 * tile), BF16),
            vmem((width, 4 * tile), BF16),
            vmem((2, 8, 4, tile // 4, part), F32),
            vmem((2, columns, 2 * part), BF16),
            vmem((2, rows, part), F32),
            vmem((2, 2, 2 * tile, part), F32),
            vmem((2, 2, 4 * tile, part), F32),
            vmem((2, 4 * tile, part), F32),
            vmem((2, 3, tile, part), F32),
            vmem((2, tile, part), F32),
            vmem((2, width, part), F32),
            vmem((2, 15, chunk, part), F32),
            vmem((2, chunk, part), F32),
            vmem((2, 8, chunk, part), F32),
            vmem((2, width, part), F32),
            vmem((2, 2 * part, part), F32),
            vmem((2, 8, tile // 4, part), F32),
            vmem((4, 4, tile, part), F32),
            dma((16,)),
            dma((5,)),
            dma((2, 7)),
            dma((2, 8)),
            dma((3,)),
            dma((4,)),
            dma((3,)),
            dma((4,)),
            dma((2, 8)),
            dma((2, 8)),
            dma((2, 6)),
            dma((2, 6)),
            dma((2, 6)),
            dma((2, 6)),
            dma((2, 3)),
            dma((2, 3)),
            dma((2, 15)),
            dma((2, 15)),
            dma((2, 7)),
            dma((2, 8)),
            dma((2, 15)),
            dma((2, 15)),
            dma((2, 16)),
            dma((2, 8)),
        ],
        compiler_params=pltpu.CompilerParams(collective_id=0, has_side_effects=True, vmem_limit_bytes=40 * 1024 * 1024),
    )(
        tile_structure.astype(F32),
        *(pltpu.with_memory_space_constraint(value, pltpu.HBM) for value in (ancestor_inverse, factor, factor_normalizer)),
    )
    return ancestor_columns, pivot_inverse - symmetric


def solution(mesh):
    return jax.shard_map(
        body,
        mesh=mesh,
        in_specs=(P("row", "col"), P("row", "col"), P(("row", "col"), None), P(), P(None, "rep")),
        out_specs=(P(("row", "col"), "rep"), P(None, "rep")),
        check_vma=False,
    )
```
